256 devices in a mesh: client: 32 (over y, x, core), shard: 8 (over z).
Axes of the slice: x: 4, y: 4, z: 8, core: 2. Of those that a mesh axis runs over, the one named last changes fastest.
Arguments:
- query_base: bfloat16 [32, 1024, 8192], P('client', 'shard'), may hold values from -3 to 3
- query_left: bfloat16 [32, 1024, 8], P('client', 'shard'), may hold values from -3 to 3
- query_right: bfloat16 [32, 8, 8192], P('client', None, 'shard'), may hold values from -3 to 3
- output_base: bfloat16 [32, 1024, 8192], P('client', 'shard'), may hold values from -3 to 3
- output_left: bfloat16 [32, 1024, 8], P('client', 'shard'), may hold values from -3 to 3
- output_right: bfloat16 [32, 8, 8192], P('client', None, 'shard'), may hold values from -3 to 3
Outputs:
- query_folded: bfloat16 [32, 1024, 8192], P('client', 'shard')
- output_folded: bfloat16 [32, 1024, 8192], P('client', 'shard')
- query_left_mean: bfloat16 [1024, 8], P('shard')
- query_right_mean: bfloat16 [8, 8192], P(None, 'shard')
- output_left_mean: bfloat16 [1024, 8], P('shard')
- output_right_mean: bfloat16 [8, 8192], P(None, 'shard')
The draws below stay inside these ranges and needn't reach their ends.
All inputs are finite; a program needn't handle non-finite values.
Results may differ from the reference program's by a relative error of at most 0.0075.
Values may be sent and summed in bfloat16 or wider, within the bound.
No kernel may reach another device: no remote copies, remote signals or barrier semaphores. Data moves between devices by JAX's collectives and lax.ppermute only.
A program may use at most 64 MiB of HBM per device.

```python
import jax
import jax.numpy as jnp

D = 8192
R = 8
ROWS = 1024
CLIENTS = 32


def level_of(rng, shape, shards, smallest, top_value):
    gain = 1.0
    for position, shards_of in shards:
        draws = jax.random.uniform(jax.random.fold_in(jax.random.fold_in(rng, 6), position), (shards_of,), jnp.float32, smallest / len(shards), top_value / len(shards))
        gain = gain * jnp.repeat(jnp.exp(draws), shape[position] // shards_of).reshape((-1,) + (1,) * (len(shape) - 1 - position))
    return gain


def bell_draw(stream_key, shape, scale, bound, split=(), held_as=jnp.bfloat16):
    values = scale * jax.random.normal(stream_key, shape, jnp.float32)
    if split:
        values = values * level_of(stream_key, shape, split, -0.22, 0.18)
    return jnp.clip(values, -bound, bound).astype(held_as)


def setup_inputs(seed: int = 0) -> dict:
    seeds = jax.random.split(jax.random.key(seed), 7)
    return {
        "query_base": bell_draw(seeds[0], (CLIENTS, ROWS, D), 0.5, 3.0, ((0, 32), (1, 8))),
        "query_left": bell_draw(seeds[1], (CLIENTS, ROWS, R), 0.5, 3.0, ((0, 32), (1, 8))),
        "query_right": bell_draw(seeds[2], (CLIENTS, R, D), 0.5, 3.0, ((0, 32), (2, 8))),
        "output_base": bell_draw(seeds[3], (CLIENTS, ROWS, D), 0.5, 3.0, ((0, 32), (1, 8))),
        "output_left": bell_draw(seeds[4], (CLIENTS, ROWS, R), 0.5, 3.0, ((0, 32), (1, 8))),
        "output_right": bell_draw(seeds[5], (CLIENTS, R, D), 0.5, 3.0, ((0, 32), (2, 8))),
    }


fold_scale = 2.0


def fold_one(base, left, right):
    count = left.shape[0]
    rows = left.shape[1]
    left_mean = (jnp.sum(left.astype(jnp.float32), 0) / count).astype(jnp.bfloat16)
    right_mean = (jnp.sum(right.astype(jnp.float32), 0) / count).astype(jnp.bfloat16)
    joined_left = jnp.transpose(left, (1, 0, 2)).reshape(rows, count * R)
    joined_right = right.reshape(count * R, right.shape[2])
    total = jnp.dot(joined_left, joined_right, preferred_element_type=jnp.float32)
    resid = (total / count - jnp.dot(left_mean, right_mean, preferred_element_type=jnp.float32)).astype(jnp.bfloat16)
    folded = (base.astype(jnp.float32) + fold_scale * resid.astype(jnp.float32)[None]).astype(jnp.bfloat16)
    return folded, left_mean, right_mean


def reference(query_base, query_left, query_right, output_base, output_left, output_right):
    query_folded, query_lm, query_rm = fold_one(query_base, query_left, query_right)
    output_folded, output_lm, output_rm = fold_one(output_base, output_left, output_right)
    return query_folded, output_folded, query_lm, query_rm, output_lm, output_rm
```

```python
import jax
import jax.numpy as jnp
from jax import lax
from jax.experimental import pallas as pl
from jax.experimental.pallas import tpu as pltpu
from jax.sharding import PartitionSpec as P

fold_scale = 2.0

SIDE = 4
CORES = 2
CLIENTS = SIDE * SIDE * CORES
SHARDS = 8
RANK = 8
ROWS = 128
COLS = 8192
BLOCK = COLS // CLIENTS
PIECE = ROWS + RANK
OFFSETS = (0, -1, 1, 2)


def client_of(y, x, core):
    return (y % SIDE) * SIDE * CORES + (x % SIDE) * CORES + core


def coords_of(client):
    return client // (SIDE * CORES), (client // CORES) % SIDE, client % CORES


def shift_pairs(step, swapped):
    pairs = []
    for client in range(CLIENTS):
        y, x, core = coords_of(client)
        if (core == 0) != swapped:
            pairs.append((client, client_of(y, x + step, core)))
        else:
            pairs.append((client, client_of(y + step, x, core)))
    return pairs


CORE_PAIRS = [(client, client ^ 1) for client in range(CLIENTS)]


def spread(piece, swapped):
    return [piece] + [
        lax.ppermute(piece, "client", shift_pairs(-offset, swapped)) for offset in OFFSETS[1:]
    ]


def piece_body(pieces_ref, piece_ref, lmean_ref):
    for p in range(2):
        rows = pl.ds(RANK * p, RANK)
        right = pieces_ref[:, rows, :BLOCK].astype(jnp.float32)
        left = pieces_ref[:, rows, BLOCK:].astype(jnp.float32)
        rmean = (jnp.sum(right, axis=0) / CLIENTS).astype(jnp.bfloat16)
        lmean = (jnp.sum(left, axis=0) / CLIENTS).astype(jnp.bfloat16)
        total = lax.dot_general(
            left.reshape(CLIENTS * RANK, ROWS).astype(jnp.bfloat16),
            right.reshape(CLIENTS * RANK, BLOCK).astype(jnp.bfloat16),
            (((0,), (0,)), ((), ())),
            preferred_element_type=jnp.float32,
        )
        product = lax.dot_general(
            lmean, rmean, (((0,), (0,)), ((), ())), preferred_element_type=jnp.float32
        )
        piece_ref[p, :ROWS, :] = (total / CLIENTS - product).astype(jnp.bfloat16)
        piece_ref[p, ROWS:, :] = rmean
        lmean_ref[p] = lmean


def make_piece(pieces):
    return pl.pallas_call(
        piece_body,
        out_shape=(
            jax.ShapeDtypeStruct((2, PIECE, BLOCK), jnp.bfloat16),
            jax.ShapeDtypeStruct((2, RANK, ROWS), jnp.bfloat16),
        ),
        compiler_params=pltpu.CompilerParams(vmem_limit_bytes=8 << 20),
        name="make_piece",
    )(pieces)


def fold_body(other, first, *refs):
    refs = list(refs)
    base = refs[:2]
    lines = refs[2:6]
    if first:
        outs = refs[6:8]
        means = refs[8:10]
        stage, sems = refs[10:]
    else:
        before = refs[8:10]
        outs = refs[10:12]
        means = refs[12:14]
        stage, sems = refs[14:]
        for p in range(2):
            means[p][...] = before[p][...]
    me = lax.axis_index("client")
    shard = lax.axis_index("shard")
    y, x, core = coords_of(me)
    if other:
        core = 1 - core
    for j, far in enumerate(OFFSETS):
        for i, near in enumerate(OFFSETS):
            dy = jnp.where(core == 0, far, near)
            dx = jnp.where(core == 0, near, far)
            block = client_of(y + dy + SIDE, x + dx + SIDE, core)
            columns = pl.ds(pl.multiple_of(block * BLOCK, BLOCK), BLOCK)
            for p in range(2):
                slot = (j * SIDE + i) * 2 + p
                resid = lines[j][i, p, :ROWS, :].astype(jnp.float32)
                stage[slot] = (
                    base[p][:, columns].astype(jnp.float32) + fold_scale * resid
                ).astype(jnp.bfloat16)
                pltpu.make_async_copy(
                    stage.at[slot], outs[p].at[:, columns], sems.at[slot]
                ).start()

            @pl.when(block // SIDE == shard)
            def _():
                at = pl.ds(pl.multiple_of((block % SIDE) * BLOCK, BLOCK), BLOCK)
                for p in range(2):
                    means[p][:, at] = lines[j][i, p, ROWS:, :]

    for j, far in enumerate(OFFSETS):
        for i, near in enumerate(OFFSETS):
            dy = jnp.where(core == 0, far, near)
            dx = jnp.where(core == 0, near, far)
            block = client_of(y + dy + SIDE, x + dx + SIDE, core)
            columns = pl.ds(pl.multiple_of(block * BLOCK, BLOCK), BLOCK)
            for p in range(2):
                slot = (j * SIDE + i) * 2 + p
                pltpu.make_async_copy(
                    stage.at[slot], outs[p].at[:, columns], sems.at[slot]
                ).wait()


def fold(base, lines, before, other):
    first = before is None
    vmem = pl.BlockSpec(memory_space=pltpu.VMEM)
    hbm = pl.BlockSpec(memory_space=pl.ANY)
    args = list(base) + list(lines)
    in_specs = [vmem] * len(args)
    aliases = {}
    if not first:
        aliases = {6: 0, 7: 1}
        args += list(before)
        in_specs += [hbm, hbm, vmem, vmem]
    slots = 2 * SIDE * SIDE
    return pl.pallas_call(
        lambda *refs: fold_body(other, first, *refs),
        out_shape=(jax.ShapeDtypeStruct((ROWS, COLS), jnp.bfloat16),) * 2
        + (jax.ShapeDtypeStruct((RANK, COLS // SHARDS), jnp.bfloat16),) * 2,
        in_specs=in_specs,
        out_specs=(hbm, hbm, vmem, vmem),
        scratch_shapes=[
            pltpu.VMEM((slots, ROWS, BLOCK), jnp.bfloat16),
            pltpu.SemaphoreType.DMA((slots,)),
        ],
        input_output_aliases=aliases,
        compiler_params=pltpu.CompilerParams(vmem_limit_bytes=16 << 20),
        name="fold_other" if other else "fold_own",
    )(*args)


def shards(query_base, query_left, query_right, output_base, output_left, output_right):
    right = jnp.stack([query_right[0], output_right[0]])
    blocks = COLS // SHARDS // BLOCK
    right = right.reshape(2, RANK, blocks, BLOCK).transpose(2, 0, 1, 3)
    right = right.reshape(1, blocks * 2 * RANK, BLOCK)
    right = lax.all_to_all(
        jnp.broadcast_to(right, (SHARDS,) + right.shape[1:]), "shard", 0, 0, tiled=True
    )
    right = right.reshape(CLIENTS, 2 * RANK, BLOCK)
    left = jnp.concatenate([query_left[0].T, output_left[0].T])
    left = jnp.broadcast_to(left[None], (CLIENTS, 2 * RANK, ROWS))
    pieces = lax.all_to_all(
        jnp.concatenate([right, left], axis=2), "client", 0, 0, tiled=True
    )
    piece, lmean = make_piece(pieces)
    near = jnp.stack(spread(piece, False))
    far = spread(near, True)
    other = [lax.ppermute(line, "client", CORE_PAIRS) for line in far]
    base = (query_base[0], output_base[0])
    folded = fold(base, far, None, False)
    folded = fold(base, other, folded, True)
    return (
        folded[0][None],
        folded[1][None],
        lmean[0].T,
        folded[2],
        lmean[1].T,
        folded[3],
    )


def solution(mesh):
    return jax.shard_map(
        shards,
        mesh=mesh,
        in_specs=(
            P("client", "shard", None),
            P("client", "shard", None),
            P("client", None, "shard"),
            P("client", "shard", None),
            P("client", "shard", None),
            P("client", None, "shard"),
        ),
        out_specs=(
            P("client", "shard", None),
            P("client", "shard", None),
            P("shard", None),
            P(None, "shard"),
            P("shard", None),
            P(None, "shard"),
        ),
        check_vma=False,
    )
```

```python
import jax
import jax.numpy as jnp
from jax import lax
from jax.experimental import pallas as pl
from jax.experimental.pallas import tpu as pltpu
from jax.sharding import PartitionSpec as P

fold_scale = 2.0

SIDE = 4
CORES = 2
CLIENTS = SIDE * SIDE * CORES
SHARDS = 8
RANK = 8
ROWS = 128
COLS = 8192
WIDTH = COLS // SHARDS
HALF = WIDTH // CORES
TILE = HALF // SIDE
CHIP = CORES * 2 * RANK
OFFSETS = (0, -1, 1, 2)


MEM = pl.BlockSpec(memory_space=pltpu.VMEM)
ANY = pl.BlockSpec(memory_space=pl.ANY)


def client_of(y, x, core):
    return (y % SIDE) * SIDE * CORES + (x % SIDE) * CORES + core


def coords_of(client):
    return client // (SIDE * CORES), (client // CORES) % SIDE, client % CORES


def place(far, near, core):
    return client_of(far, near, core) if core == 0 else client_of(near, far, core)


def far_of(core):
    y, x, _ = coords_of(lax.axis_index("client"))
    return jnp.where(core == 0, y, x)


def shift_pairs(step, along_far):
    pairs = []
    for core in range(CORES):
        for far in range(SIDE):
            for near in range(SIDE):
                to = (far + step, near) if along_far else (far, near + step)
                pairs.append((place(far, near, core), place(*to, core)))
    return pairs


CORE_PAIRS = [(client, client ^ 1) for client in range(CLIENTS)]
LINES = [
    [place(far, near, core) * SHARDS + shard for shard in range(SHARDS) for far in range(SIDE)]
    for core in range(CORES)
    for near in range(SIDE)
]


def spread(piece, along_far):
    return [piece] + [
        lax.ppermute(piece, "client", shift_pairs(-offset, along_far)) for offset in OFFSETS[1:]
    ]


def give_body(*refs):
    rights, lefts, outs, sems = refs[:2], refs[2:4], refs[4:6], refs[6]
    core = lax.axis_index("client") % CORES
    copies = []
    for o, half in enumerate((core, 1 - core)):
        columns = pl.ds(pl.multiple_of(half * HALF, HALF), HALF)
        for p in range(2):
            rows = pl.ds(RANK * p, RANK)
            copies.append((rights[p].at[:, columns], outs[o].at[rows, pl.ds(0, HALF)]))
            copies.append((lefts[p], outs[o].at[rows, pl.ds(HALF, ROWS)]))
    copies = [pltpu.make_async_copy(*pair, sems.at[i]) for i, pair in enumerate(copies)]
    for copy in copies:
        copy.start()
    for copy in copies:
        copy.wait()


def give_half(rights, lefts):
    shape = jax.ShapeDtypeStruct((2 * RANK, HALF + ROWS), jnp.bfloat16)
    return pl.pallas_call(
        give_body,
        out_shape=(shape, shape),
        in_specs=[ANY] * 4,
        out_specs=(MEM, MEM),
        scratch_shapes=[pltpu.SemaphoreType.DMA((8,))],
        compiler_params=pltpu.CompilerParams(vmem_limit_bytes=4 << 20),
        name="give_half",
    )(*rights, *lefts)


def split_body(kept, taken, right_out, left_out):
    for p in range(2):
        rows = slice(RANK * p, RANK * (p + 1))
        for c, half in enumerate((kept, taken)):
            at = slice(RANK * (2 * c + p), RANK * (2 * c + p + 1))
            left_out[at, :] = half[rows, HALF:]
            for far in range(SIDE):
                tile = half[rows, far * TILE : (far + 1) * TILE]
                for shard in range(SHARDS):
                    right_out[shard * SIDE + far, at, :] = tile


def split_half(kept, taken):
    return pl.pallas_call(
        split_body,
        out_shape=(
            jax.ShapeDtypeStruct((SHARDS * SIDE, CHIP, TILE), jnp.bfloat16),
            jax.ShapeDtypeStruct((CHIP, ROWS), jnp.bfloat16),
        ),
        in_specs=[MEM] * 2,
        out_specs=(MEM, MEM),
        compiler_params=pltpu.CompilerParams(vmem_limit_bytes=4 << 20),
        name="split_half",
    )(kept, taken)


def piece_body(*refs):
    lines, (piece, lmean_out) = refs[:SIDE], refs[SIDE:]
    shard = lax.axis_index("shard")
    far = far_of(lax.axis_index("client") % CORES)
    fars = [(far + offset + SIDE) % SIDE for offset in OFFSETS]

    def parts(entries, p):
        out = []
        for line in lines:
            for entry in entries:
                chip = line[entry].astype(jnp.float32)
                for core in range(CORES):
                    start = (core * 2 + p) * RANK
                    out.append(chip[start : start + RANK])
        return out

    def mean(values):
        while len(values) > 1:
            values = [a + b for a, b in zip(values[::2], values[1::2])]
        return (values[0] / CLIENTS).astype(jnp.bfloat16)

    def contract(left, right):
        return lax.dot_general(
            left, right, (((0,), (0,)), ((), ())), preferred_element_type=jnp.float32
        )

    for p in range(2):
        left = parts([SHARDS * SIDE + j for j in range(SIDE)], p)
        lmean = mean(left)
        lmean_out[p] = lmean
        left = jnp.concatenate(left, axis=0).astype(jnp.bfloat16)
        rights = []
        rmeans = []
        for z in range(SHARDS):
            right = parts([z * SIDE + f for f in fars], p)
            rmeans.append(mean(right))
            rights.append(jnp.concatenate(right, axis=0).astype(jnp.bfloat16))
        total = contract(left, jnp.concatenate(rights, axis=1))
        product = contract(lmean, jnp.concatenate(rmeans, axis=1))
        resid = (total / CLIENTS - product).astype(jnp.bfloat16)
        for z in range(SHARDS):
            start = (p * SHARDS + z) * ROWS
            piece[start : start + ROWS, :] = resid[:, z * TILE : (z + 1) * TILE]

            @pl.when(z == shard)
            def _():
                start = 2 * SHARDS * ROWS + p * RANK
                piece[start : start + RANK, :] = rmeans[z]


def make_piece(lines):
    return pl.pallas_call(
        piece_body,
        out_shape=(
            jax.ShapeDtypeStruct((2 * SHARDS * ROWS + 2 * RANK, TILE), jnp.bfloat16),
            jax.ShapeDtypeStruct((2, RANK, ROWS), jnp.bfloat16),
        ),
        in_specs=[MEM] * SIDE,
        out_specs=(MEM, MEM),
        compiler_params=pltpu.CompilerParams(vmem_limit_bytes=12 << 20),
        name="make_piece",
    )(*lines)


def fold_body(other, first, *refs):
    base = refs[:2]
    lines = refs[2:6]
    if first:
        outs = refs[6:8]
        means = refs[8:10]
        stage, sems = refs[10:]
    else:
        before = refs[8:10]
        outs = refs[10:12]
        means = refs[12:14]
        stage, sems = refs[14:]
        for p in range(2):
            means[p][...] = before[p][...]
    core = lax.axis_index("client") % CORES
    if other:
        core = 1 - core
    far = far_of(core)
    copies = []
    for j, offset in enumerate(OFFSETS):
        within = core * HALF + (far + offset + SIDE) % SIDE * TILE
        for z in range(SHARDS):
            columns = pl.ds(pl.multiple_of(z * WIDTH + within, TILE), TILE)
            for p in range(2):
                slot = (j * SHARDS + z) * 2 + p
                start = (p * SHARDS + z) * ROWS
                resid = lines[j][start : start + ROWS, :].astype(jnp.float32)
                stage[slot] = (
                    base[p][:, columns].astype(jnp.float32) + fold_scale * resid
                ).astype(jnp.bfloat16)
                copy = pltpu.make_async_copy(
                    stage.at[slot], outs[p].at[:, columns], sems.at[slot]
                )
                copy.start()
                copies.append(copy)
        at = pl.ds(pl.multiple_of(within, TILE), TILE)
        for p in range(2):
            start = 2 * SHARDS * ROWS + p * RANK
            means[p][:, at] = lines[j][start : start + RANK, :]
    for copy in copies:
        copy.wait()


def fold(base, lines, before, other):
    first = before is None
    args = list(base) + list(lines)
    in_specs = [MEM] * len(args)
    aliases = {}
    if not first:
        aliases = {6: 0, 7: 1}
        args += list(before)
        in_specs += [ANY, ANY, MEM, MEM]
    slots = 2 * SHARDS * SIDE
    return pl.pallas_call(
        lambda *refs: fold_body(other, first, *refs),
        out_shape=(jax.ShapeDtypeStruct((ROWS, COLS), jnp.bfloat16),) * 2
        + (jax.ShapeDtypeStruct((RANK, WIDTH), jnp.bfloat16),) * 2,
        in_specs=in_specs,
        out_specs=(ANY, ANY, MEM, MEM),
        scratch_shapes=[
            pltpu.VMEM((slots, ROWS, TILE), jnp.bfloat16),
            pltpu.SemaphoreType.DMA((slots,)),
        ],
        input_output_aliases=aliases,
        compiler_params=pltpu.CompilerParams(vmem_limit_bytes=16 << 20),
        name="fold_other" if other else "fold_own",
    )(*args)


def shards(query_base, query_left, query_right, output_base, output_left, output_right):
    rights = (query_right[0], output_right[0])
    lefts = (query_left[0].T, output_left[0].T)
    kept, given = give_half(rights, lefts)
    right, left = split_half(kept, lax.ppermute(given, "client", CORE_PAIRS))
    left = jnp.stack(spread(left, True))
    right = lax.all_to_all(
        right, ("client", "shard"), 0, 0, tiled=True, axis_index_groups=LINES
    )
    near = spread(jnp.concatenate([right, left]), False)
    piece, lmean = make_piece(near)
    far = spread(piece, True)
    other = [lax.ppermute(line, "client", CORE_PAIRS) for line in far]
    base = (query_base[0], output_base[0])
    folded = fold(base, far, None, False)
    folded = fold(base, other, folded, True)
    return (
        folded[0][None],
        folded[1][None],
        lmean[0].T,
        folded[2],
        lmean[1].T,
        folded[3],
    )


def solution(mesh):
    return jax.shard_map(
        shards,
        mesh=mesh,
        in_specs=(
            P("client", "shard", None),
            P("client", "shard", None),
            P("client", None, "shard"),
            P("client", "shard", None),
            P("client", "shard", None),
            P("client", None, "shard"),
        ),
        out_specs=(
            P("client", "shard", None),
            P("client", "shard", None),
            P("shard", None),
            P(None, "shard"),
            P("shard", None),
            P(None, "shard"),
        ),
        check_vma=False,
    )
```
